256 devices in a mesh: tm: 8 (over x_hi, y), gx: 32 (over z, x_lo, core).
Axes of the slice: x: 4 (x_hi: 2, x_lo: 2; x = x_hi * 2 + x_lo), y: 4, z: 8, core: 2. Of those that a mesh axis runs over, the one named last changes fastest.
Arguments:
- start_states: float32 [8, 512, 128, 128], P('tm', 'gx'), may hold values from -1.2 to 1.2
- mobility: float32 [512, 128, 128], P('gx'), may hold values from 0.25 to 1
Outputs:
- end_state: float32 [8, 512, 128, 128], P('tm', 'gx')
- next_start: float32 [8, 512, 128, 128], P('tm', 'gx')
The draws below stay inside these ranges and needn't reach their ends.
All inputs are finite; a program needn't handle non-finite values.
Results may differ from the reference program's by a relative error of at most 0.0001.
Values sent between devices are 32-bit elements; how exact they have to be, the bound alone decides.
A program may use at most 128 MiB of HBM per device.

```python
import math
import jax
import jax.numpy as jnp
from jax import lax

NY = 128
NZ = 128
KY = 64
KZ = 64
ITERS = 2
NX = 512
SLICES = 8


def block_levels(stream_key, extent, shards, low, high):
    level = 1.0
    for dim, parts in shards:
        heights = jax.random.uniform(jax.random.fold_in(jax.random.fold_in(stream_key, 6), dim), (parts,), jnp.float32, low / len(shards), high / len(shards))
        level = level * jnp.repeat(jnp.exp(heights), extent[dim] // parts).reshape((-1,) + (1,) * (len(extent) - 1 - dim))
    return level


def setup_inputs(seed: int = 0) -> dict:
    arg_keys = jax.random.split(jax.random.key(seed), 3)
    start_states = jnp.clip(jax.random.uniform(arg_keys[0], (SLICES, NX, NY, NZ), jnp.float32, -1.2, 1.2) * block_levels(arg_keys[0], (SLICES, NX, NY, NZ), ((0, 8), (1, 32)), -0.4, 0.0), -1.2, 1.2)
    mobility = jnp.clip(jnp.exp(math.log(1.0) - 1.3862944 * jax.random.uniform(arg_keys[1], (NX, NY, NZ), jnp.float32) ** block_levels(arg_keys[1], (NX, NY, NZ), ((0, 32),), -0.2, 0.2)), 0.25, 1.0)
    return {"start_states": start_states, "mobility": mobility}


time_step = 0.05

def basis_value(node_times, source, point):
    total = 1.0
    for other in range(5):
        if other != source:
            total = total * (point - node_times[other]) / (node_times[source] - node_times[other])
    return total

def picard_table():
    root = math.sqrt(3.0 / 7.0)
    node_times = [0.0, (1.0 - root) / 2.0, 0.5, (1.0 + root) / 2.0, 1.0]
    gauss_points = [-math.sqrt(0.6), 0.0, math.sqrt(0.6)]
    gauss_weights = [5.0 / 9.0, 8.0 / 9.0, 5.0 / 9.0]
    picard_rows = []
    for target in range(1, 5):
        upper = node_times[target]
        row_values = []
        for source in range(5):
            integral = 0.0
            for point, weight in zip(gauss_points, gauss_weights):
                integral = integral + 0.5 * upper * weight * basis_value(node_times, source, 0.5 * upper * (1.0 + point))
            row_values.append(integral)
        picard_rows.append(row_values)
    return picard_rows

def dct_rows(count, kept):
    freq = jnp.arange(kept, dtype=jnp.float32)[:, None]
    place = jnp.arange(count, dtype=jnp.float32)[None, :]
    matrix = jnp.cos(jnp.pi * (place + 0.5) * freq / count) * jnp.sqrt(2.0 / count)
    return jnp.where(freq == 0, matrix * jnp.sqrt(0.5), matrix)

def project(values):
    low_y = dct_rows(NY, KY)
    low_z = dct_rows(NZ, KZ)
    hp = lax.Precision.HIGHEST
    coeffs = jnp.einsum('ky,...yz->...kz', low_y, values, precision=hp)
    coeffs = jnp.einsum('...kz,lz->...kl', coeffs, low_z, precision=hp)
    back = jnp.einsum('...kl,lz->...kz', coeffs, low_z, precision=hp)
    return jnp.einsum('ky,...kz->...yz', low_y, back, precision=hp)

def evaluate(fields, mobility):
    padded = jnp.pad(fields, ((0, 0), (1, 1), (1, 1), (1, 1)))
    values = padded[:, 1:-1, 1:-1, 1:-1]
    laplace = padded[:, 2:, 1:-1, 1:-1] + padded[:, :-2, 1:-1, 1:-1]
    laplace = laplace + padded[:, 1:-1, 2:, 1:-1] + padded[:, 1:-1, :-2, 1:-1]
    laplace = laplace + padded[:, 1:-1, 1:-1, 2:] + padded[:, 1:-1, 1:-1, :-2] - 6.0 * values
    return mobility * (laplace + values - values * values * values)

def reference(start_states, mobility):
    picard_rows = picard_table()

    def sweep(pair):
        start_value, nodes = pair
        fields = jnp.concatenate([start_value[None], nodes], axis=0)
        node_rates = evaluate(fields, mobility)
        updated = []
        for target in range(4):
            total = picard_rows[target][0] * node_rates[0]
            for source in range(1, 5):
                total = total + picard_rows[target][source] * node_rates[source]
            updated.append(start_value + time_step * total)
        return jnp.stack(updated, axis=0)
    start_value = start_states
    nodes = jnp.broadcast_to(start_states[:, None], (start_states.shape[0], 4) + start_states.shape[1:])
    end_value = start_states
    for iteration in range(ITERS):
        nodes = lax.map(sweep, (start_value, nodes))
        end_value = nodes[:, 3]
        arrived = jnp.concatenate([jnp.zeros_like(end_value[:1]), end_value[:-1]], axis=0)
        receive_mask = (jnp.arange(start_value.shape[0]) > 0).astype(jnp.float32)[:, None, None, None]
        start_value = start_value + receive_mask * lax.map(project, arrived - start_value)
    return (end_value, start_value)
```

```python
import functools
import math

import jax
import jax.numpy as jnp
import ml_dtypes
import numpy as np
from jax import lax
from jax.experimental import pallas as pl
from jax.experimental.pallas import tpu as pltpu
from jax.sharding import PartitionSpec as P

KY = 64
KZ = 64
NY = 128
NZ = 128
time_step = 0.05
MESH = pl.DeviceIdType.MESH

FIRST = (1, 0, 3, 2)
SECOND = ((1, 2, 3, 4), (7, 8, 9, 10), (11, 12, 13, 14), (5, 6, 0, 15))


def basis_value(node_times, source, point):
    total = 1.0
    for other in range(5):
        if other != source:
            total = total * (point - node_times[other]) / (node_times[source] - node_times[other])
    return total


def picard_table():
    root = math.sqrt(3.0 / 7.0)
    node_times = [0.0, (1.0 - root) / 2.0, 0.5, (1.0 + root) / 2.0, 1.0]
    gauss_points = [-math.sqrt(0.6), 0.0, math.sqrt(0.6)]
    gauss_weights = [5.0 / 9.0, 8.0 / 9.0, 5.0 / 9.0]
    picard_rows = []
    for target in range(1, 5):
        upper = node_times[target]
        row_values = []
        for source in range(5):
            integral = 0.0
            for point, weight in zip(gauss_points, gauss_weights):
                integral = integral + 0.5 * upper * weight * basis_value(
                    node_times, source, 0.5 * upper * (1.0 + point)
                )
            row_values.append(integral)
        picard_rows.append(row_values)
    return picard_rows


def sweep_weights():
    rows = picard_table()
    last = rows[3]
    reach = [time_step * sum(row) for row in rows]
    moments = [sum(last[j] * reach[j - 1] ** k for j in range(1, 5)) for k in range(4)]
    return reach[3], last[0], moments


def dct_rows(count, kept):
    freq = np.arange(kept, dtype=np.float64)[:, None]
    place = np.arange(count, dtype=np.float64)[None, :]
    matrix = np.cos(np.pi * (place + 0.5) * freq / count) * np.sqrt(2.0 / count)
    return np.where(freq == 0, matrix * np.sqrt(0.5), matrix)


def two_parts(matrix):
    high = matrix.astype(ml_dtypes.bfloat16)
    low = (matrix - high.astype(np.float64)).astype(ml_dtypes.bfloat16)
    return high, low


def on_diagonal(block):
    zero = np.zeros_like(block)
    return np.block([[block, zero], [zero, block]])


LA, BA, DS, LS, PY, PZ, ROWS = 0, 128, 384, 768, 896, 1152, 1408


def tables():
    cy, cz = dct_rows(NY, KY), dct_rows(NZ, KZ)
    yh, yl = two_parts(cy)
    zh, zl = two_parts(cz)
    pyh, pyl = two_parts(cy.T @ cy)
    pzh, pzl = two_parts(cz.T @ cz)
    dh, dl = on_diagonal(zh), on_diagonal(zl)
    parts = [
        np.block([[yh, yh], [yl, yl]]),
        np.concatenate([dh.T, dl.T], axis=1),
        np.concatenate([dh, dh, dl], axis=0),
        np.concatenate([yh.T, yh.T, yl.T, yl.T], axis=1),
        np.block([[pyh, pyh], [pyl, pyl]]),
        np.block([[pzh, pzl], [pzh, pzl]]),
    ]
    return np.concatenate(parts, axis=0).astype(ml_dtypes.bfloat16)


def halves(value):
    high = value.astype(jnp.bfloat16)
    low = (value - high.astype(jnp.float32)).astype(jnp.bfloat16)
    return high, low


def mul(left, right):
    return jnp.dot(left, right, preferred_element_type=jnp.float32)


def analyse_pair(first, second, tab):
    high, low = halves(jnp.concatenate([first, second], axis=1))
    out = mul(tab[LA : LA + 128, :], jnp.concatenate([high, low], axis=0))
    return out[:64] + out[64:]


def analyse(planes, tab):
    rows = jnp.concatenate(
        [analyse_pair(planes[0], planes[1], tab), analyse_pair(planes[2], planes[3], tab)], axis=0
    )
    high, low = halves(rows)
    out = mul(jnp.concatenate([high, low], axis=0), tab[BA : BA + 256, :])
    return (out[:128, :128] + out[128:, :128]) + (out[:128, 128:] + out[128:, 128:])


def synthesise(block, tab):
    high, low = halves(block)
    rows = mul(jnp.concatenate([high, low, high], axis=1), tab[DS : DS + 384, :])
    planes = []
    for pair in range(2):
        high, low = halves(rows[64 * pair : 64 * pair + 64])
        out = mul(tab[LS : LS + 128, :], jnp.concatenate([high, low, high, low], axis=0))
        planes += [out[:, :128], out[:, 128:]]
    return planes


def smooth_pair(first, second, tab):
    high, low = halves(jnp.concatenate([first, second], axis=1))
    out = mul(tab[PY : PY + 256, :], jnp.concatenate([high, low], axis=0))
    out = out[:128] + out[128:]
    high, low = halves(jnp.concatenate([out[:, :128], out[:, 128:]], axis=0))
    out = mul(jnp.concatenate([high, low], axis=1), tab[PZ : PZ + 256, :])
    out = out[:, :128] + out[:, 128:]
    return out[:128], out[128:]


def kernel(
    a_hbm, mob_hbm, tab_hbm, end_hbm, next_hbm,
    a_v, mob_v, tab, f_v, w_v, r_v, ap_v, e_v, n_v, e1_v, cs, cr,
    in_sem, out_sem, ss, rs, hs, hr,
):
    t = lax.axis_index("tm")
    g = lax.axis_index("gx")
    g_count = lax.axis_size("gx")
    t_count = lax.axis_size("tm")
    has_left, has_right = g > 0, g < g_count - 1
    has_prev, has_next = t > 0, t < t_count - 1
    reach, q0, (s0, s1, s2, s3) = sweep_weights()

    loads = []
    for k, c in enumerate((0, 1, 2, 3)):
        loads.append(pltpu.make_async_copy(a_hbm.at[0, pl.ds(4 * c, 4)], a_v.at[pl.ds(1 + 4 * c, 4)], in_sem.at[c]))
    mob_loads = [
        pltpu.make_async_copy(mob_hbm.at[pl.ds(4 * c, 4)], mob_v.at[pl.ds(4 * c, 4)], in_sem.at[4 + c])
        for c in range(4)
    ]
    tab_loads = [
        pltpu.make_async_copy(tab_hbm.at[pl.ds(0, DS)], tab.at[pl.ds(0, DS)], in_sem.at[8]),
        pltpu.make_async_copy(tab_hbm.at[pl.ds(DS, ROWS - DS)], tab.at[pl.ds(DS, ROWS - DS)], in_sem.at[9]),
    ]
    for copy in (loads[0], loads[1], loads[2], mob_loads[1], loads[3], tab_loads[0], mob_loads[0], mob_loads[3], mob_loads[2], tab_loads[1]):
        copy.start()

    barrier = pltpu.get_barrier_semaphore()
    for present, axis, index in (
        (has_left, "gx", g - 1), (has_right, "gx", g + 1), (has_prev, "tm", t - 1), (has_next, "tm", t + 1),
    ):
        @pl.when(present)
        def _():
            pl.semaphore_signal(barrier, inc=1, device_id={axis: index}, device_id_type=MESH)

    zero = jnp.zeros((128, 128), jnp.float32)

    @pl.when(g == 0)
    def _():
        a_v[0] = zero
        w_v[0] = zero

    @pl.when(g == g_count - 1)
    def _():
        a_v[17] = zero
        w_v[17] = zero

    @pl.when(t == 0)
    def _():
        for stage in range(2):
            for c in range(4):
                cr[stage, c] = zero

    row = lax.broadcasted_iota(jnp.int32, (128, 128), 0)
    lane = lax.broadcasted_iota(jnp.int32, (128, 128), 1)

    def neighbours(ref, p):
        v = ref[p + 1]
        total = ref[p] + ref[p + 2]
        total = total + jnp.where(row == 0, 0.0, pltpu.roll(v, 1, 0))
        total = total + jnp.where(row == 127, 0.0, pltpu.roll(v, 127, 0))
        total = total + jnp.where(lane == 0, 0.0, pltpu.roll(v, 1, 1))
        total = total + jnp.where(lane == 127, 0.0, pltpu.roll(v, 127, 1))
        return total, v

    def first_rates(c):
        def step(i, carry):
            p = 4 * c + i
            total, v = neighbours(a_v, p)
            rate = mob_v[p] * (total - v * (5.0 + v * v))
            f_v[p] = rate
            e1_v[i] = v + reach * rate
            return carry

        lax.fori_loop(0, 4, step, 0)

    def send(stage, k):
        return pltpu.make_async_remote_copy(
            src_ref=cs.at[stage, k], dst_ref=cr.at[stage, k], send_sem=ss.at[stage, k], recv_sem=rs.at[stage, k],
            device_id={"tm": t + 1}, device_id_type=MESH,
        )

    def halo(ref, stage, side):
        return pltpu.make_async_remote_copy(
            src_ref=ref.at[1 if side == 0 else 16], dst_ref=ref.at[17 if side == 0 else 0],
            send_sem=hs.at[stage, side], recv_sem=hr.at[stage, side],
            device_id={"gx": g - 1 if side == 0 else g + 1}, device_id_type=MESH,
        )

    def start_halo(ref, stage, side):
        @pl.when(has_left if side == 0 else has_right)
        def _():
            halo(ref, stage, side).start()

    def take_halo(ref, stage, side):
        @pl.when(has_right if side == 0 else has_left)
        def _():
            halo(ref, stage, side).wait_recv()

    def forward(stage, k, planes):
        cs[stage, k] = analyse(planes, tab)

        @pl.when(has_next)
        def _():
            send(stage, k).start()

    def arrive(stage, k):
        @pl.when(has_prev)
        def _():
            send(stage, k).wait_recv()

    for c in range(4):
        loads[c].wait()
    mob_loads[1].wait()
    first_rates(1)
    pl.semaphore_wait(
        barrier,
        has_left.astype(jnp.int32) + has_right.astype(jnp.int32) + has_prev.astype(jnp.int32) + has_next.astype(jnp.int32),
    )
    start_halo(a_v, 0, 0)
    start_halo(a_v, 0, 1)
    tab_loads[0].wait()
    forward(0, 1, [e1_v[i] for i in range(4)])
    mob_loads[0].wait()
    take_halo(a_v, 0, 1)
    first_rates(0)
    forward(0, 0, [e1_v[i] for i in range(4)])
    mob_loads[3].wait()
    take_halo(a_v, 0, 0)
    first_rates(3)
    forward(0, 3, [e1_v[i] for i in range(4)])
    mob_loads[2].wait()
    first_rates(2)
    forward(0, 2, [e1_v[i] for i in range(4)])

    tab_loads[1].wait()
    receives = has_prev.astype(jnp.float32)

    def rest(i, carry):
        p = 2 * i
        first, second = a_v[p + 1], a_v[p + 2]
        low_first, low_second = smooth_pair(first, second, tab)
        r_v[p] = first - receives * low_first
        r_v[p + 1] = second - receives * low_second
        return carry

    lax.fori_loop(0, 8, rest, 0)

    def corrected(c):
        arrive(0, c)
        for i, plane in enumerate(synthesise(cr[0, c], tab)):
            p = 4 * c + i
            start = r_v[p] + plane
            ap_v[p] = start
            w_v[p + 1] = q0 * start + s0 * a_v[p + 1] + s1 * f_v[p]

    def second_values(low, count):
        def step(i, carry):
            p = low + i
            total, w = neighbours(w_v, p)
            a, f, start = a_v[p + 1], f_v[p], ap_v[p]
            square = a * a
            cubes = (s3 * f + (3.0 * s2) * a) * f + (3.0 * s1) * square
            cubes = cubes * f + s0 * (square * a) + q0 * (start * start * start)
            e_v[p] = start + (time_step * mob_v[p]) * ((total - 5.0 * w) - cubes)
            return carry

        lax.fori_loop(0, count, step, 0)

    def store_end(low, count, k):
        return pltpu.make_async_copy(e_v.at[pl.ds(low, count)], end_hbm.at[0, pl.ds(low, count)], out_sem.at[k])

    corrected(1)
    corrected(0)
    start_halo(w_v, 1, 0)
    second_values(1, 6)
    forward(1, 0, [e_v[p] for p in SECOND[0]])
    corrected(3)
    start_halo(w_v, 1, 1)
    corrected(2)
    second_values(7, 4)
    forward(1, 1, [e_v[p] for p in SECOND[1]])
    second_values(11, 4)
    forward(1, 2, [e_v[p] for p in SECOND[2]])
    take_halo(w_v, 1, 1)
    second_values(0, 1)
    take_halo(w_v, 1, 0)
    second_values(15, 1)
    forward(1, 3, [e_v[p] for p in SECOND[3]])
    store_end(0, 16, 0).start()

    def store_next(low, count, k):
        return pltpu.make_async_copy(n_v.at[pl.ds(low, count)], next_hbm.at[0, pl.ds(low, count)], out_sem.at[k])

    stores = [store_end(0, 16, 0)]
    pieces = (((1, 4),), ((7, 4),), ((11, 4),), ((5, 2), (0, 1), (15, 1)))
    for k in range(4):
        arrive(1, k)
        for p, plane in zip(SECOND[k], synthesise(cr[1, k], tab)):
            n_v[p] = r_v[p] + plane
        for low, count in pieces[k]:
            stores.append(store_next(low, count, len(stores)))
            stores[-1].start()

    for stage in range(2):
        @pl.when(has_next)
        def _():
            for k in range(4):
                send(stage, k).wait_send()

        ref = (a_v, w_v)[stage]

        @pl.when(has_left)
        def _():
            halo(ref, stage, 0).wait_send()

        @pl.when(has_right)
        def _():
            halo(ref, stage, 1).wait_send()
    for copy in stores:
        copy.wait()


def body(start_states, mobility):
    plane = (128, 128)
    f32 = jnp.float32
    out = jax.ShapeDtypeStruct(start_states.shape, f32)
    return pl.pallas_call(
        kernel,
        out_shape=(out, out),
        in_specs=[pl.BlockSpec(memory_space=pl.ANY)] * 3,
        out_specs=[pl.BlockSpec(memory_space=pl.ANY)] * 2,
        scratch_shapes=[
            pltpu.VMEM((18,) + plane, f32),
            pltpu.VMEM((16,) + plane, f32),
            pltpu.VMEM((ROWS, 256), jnp.bfloat16),
            pltpu.VMEM((16,) + plane, f32),
            pltpu.VMEM((18,) + plane, f32),
            pltpu.VMEM((16,) + plane, f32),
            pltpu.VMEM((16,) + plane, f32),
            pltpu.VMEM((16,) + plane, f32),
            pltpu.VMEM((16,) + plane, f32),
            pltpu.VMEM((4,) + plane, f32),
            pltpu.VMEM((2, 4) + plane, f32),
            pltpu.VMEM((2, 4) + plane, f32),
            pltpu.SemaphoreType.DMA((10,)),
            pltpu.SemaphoreType.DMA((8,)),
            pltpu.SemaphoreType.DMA((2, 4)),
            pltpu.SemaphoreType.DMA((2, 4)),
            pltpu.SemaphoreType.DMA((2, 2)),
            pltpu.SemaphoreType.DMA((2, 2)),
        ],
        compiler_params=pltpu.CompilerParams(
            collective_id=0, has_side_effects=True, vmem_limit_bytes=24 * 1024 * 1024
        ),
    )(start_states, mobility, jnp.asarray(tables()))


def solution(mesh):
    placed = (P("tm", "gx", None, None), P("gx", None, None))
    return jax.shard_map(
        body,
        mesh=mesh,
        in_specs=placed,
        out_specs=(P("tm", "gx", None, None), P("tm", "gx", None, None)),
        check_vma=False,
    )
```

```python
import math

import jax
import jax.numpy as jnp
import ml_dtypes
import numpy as np
from jax import lax
from jax.experimental import pallas as pl
from jax.experimental.pallas import tpu as pltpu
from jax.sharding import PartitionSpec as P

KY = 64
KZ = 64
NY = 128
NZ = 128
time_step = 0.05
MESH = pl.DeviceIdType.MESH

FIRST = (7, 6, 5, 4, 0, 3, 2, 1)
SECOND = (7, 6, 5, 4, 3, 2, 1, 0)


def basis_value(node_times, source, point):
    total = 1.0
    for other in range(5):
        if other != source:
            total = total * (point - node_times[other]) / (node_times[source] - node_times[other])
    return total


def picard_table():
    root = math.sqrt(3.0 / 7.0)
    node_times = [0.0, (1.0 - root) / 2.0, 0.5, (1.0 + root) / 2.0, 1.0]
    gauss_points = [-math.sqrt(0.6), 0.0, math.sqrt(0.6)]
    gauss_weights = [5.0 / 9.0, 8.0 / 9.0, 5.0 / 9.0]
    picard_rows = []
    for target in range(1, 5):
        upper = node_times[target]
        row_values = []
        for source in range(5):
            integral = 0.0
            for point, weight in zip(gauss_points, gauss_weights):
                integral = integral + 0.5 * upper * weight * basis_value(
                    node_times, source, 0.5 * upper * (1.0 + point)
                )
            row_values.append(integral)
        picard_rows.append(row_values)
    return picard_rows


def sweep_weights():
    rows = picard_table()
    last = rows[3]
    reach = [time_step * sum(row) for row in rows]
    moments = [sum(last[j] * reach[j - 1] ** k for j in range(1, 5)) for k in range(4)]
    return reach[3], last[0], moments


def dct_rows(count, kept):
    freq = np.arange(kept, dtype=np.float64)[:, None]
    place = np.arange(count, dtype=np.float64)[None, :]
    matrix = np.cos(np.pi * (place + 0.5) * freq / count) * np.sqrt(2.0 / count)
    return np.where(freq == 0, matrix * np.sqrt(0.5), matrix)


def two_parts(matrix):
    high = matrix.astype(ml_dtypes.bfloat16)
    low = (matrix - high.astype(np.float64)).astype(ml_dtypes.bfloat16)
    return high, low


def on_diagonal(block):
    zero = np.zeros_like(block)
    return np.block([[block, zero], [zero, block]])


LA, BA, DS, LS, ROWS = 0, 128, 384, 768, 896


def tables():
    yh, yl = two_parts(dct_rows(NY, KY))
    zh, zl = two_parts(dct_rows(NZ, KZ))
    dh, dl = on_diagonal(zh), on_diagonal(zl)
    parts = [
        np.block([[yh, yh], [yl, yl]]),
        np.concatenate([dh.T, dl.T], axis=1),
        np.concatenate([dh, dh, dl], axis=0),
        np.concatenate([yh.T, yh.T, yl.T, yl.T], axis=1),
    ]
    return np.concatenate(parts, axis=0).astype(ml_dtypes.bfloat16)


def halves(value):
    high = value.astype(jnp.bfloat16)
    low = (value - high.astype(jnp.float32)).astype(jnp.bfloat16)
    return high, low


def mul(left, right):
    return jnp.dot(left, right, preferred_element_type=jnp.float32)


def analyse(first, second, tab):
    high, low = halves(jnp.concatenate([first, second], axis=1))
    out = mul(tab[LA : LA + 128, :], jnp.concatenate([high, low], axis=0))
    high, low = halves(out[:64] + out[64:])
    out = mul(jnp.concatenate([high, low], axis=0), tab[BA : BA + 256, :])
    return (out[:64, :128] + out[64:, :128]) + (out[:64, 128:] + out[64:, 128:])


def synthesise(block, tab):
    high, low = halves(block)
    rows = mul(jnp.concatenate([high, low, high], axis=1), tab[DS : DS + 384, :])
    high, low = halves(rows)
    out = mul(tab[LS : LS + 128, :], jnp.concatenate([high, low, high, low], axis=0))
    return out[:, :128], out[:, 128:]


def kernel(
    a_hbm, mob_hbm, tab_hbm, e_v, n_v,
    a_v, mob_v, tab, f_v, w_v, ap_v, e1_v, ca, cs, cr,
    in_sem, ss, rs, hs, hr,
):
    t = lax.axis_index("tm")
    g = lax.axis_index("gx")
    g_count = lax.axis_size("gx")
    t_count = lax.axis_size("tm")
    has_left, has_right = g > 0, g < g_count - 1
    has_prev, has_next = t > 0, t < t_count - 1
    reach, q0, (s0, s1, s2, s3) = sweep_weights()
    receives = has_prev.astype(jnp.float32)

    a_loads = [
        pltpu.make_async_copy(a_hbm.at[0, pl.ds(4 * c, 4)], a_v.at[pl.ds(1 + 4 * c, 4)], in_sem.at[c]) for c in range(4)
    ]
    mob_loads = [
        pltpu.make_async_copy(mob_hbm.at[pl.ds(4 * c, 4)], mob_v.at[pl.ds(4 * c, 4)], in_sem.at[4 + c])
        for c in range(4)
    ]
    tab_load = pltpu.make_async_copy(tab_hbm, tab, in_sem.at[8])
    for copy in (
        a_loads[1], a_loads[2], a_loads[0], a_loads[3], mob_loads[1], mob_loads[2], tab_load, mob_loads[0], mob_loads[3],
    ):
        copy.start()

    barrier = pltpu.get_barrier_semaphore()
    for present, axis, index in (
        (has_left, "gx", g - 1), (has_right, "gx", g + 1), (has_prev, "tm", t - 1), (has_next, "tm", t + 1),
    ):
        @pl.when(present)
        def _():
            pl.semaphore_signal(barrier, inc=1, device_id={axis: index}, device_id_type=MESH)

    zero = jnp.zeros((128, 128), jnp.float32)

    @pl.when(g == 0)
    def _():
        a_v[0] = zero
        w_v[0] = zero

    @pl.when(g == g_count - 1)
    def _():
        a_v[17] = zero
        w_v[17] = zero

    @pl.when(t == 0)
    def _():
        for stage in range(2):
            for k in range(8):
                cr[stage, k] = jnp.zeros((64, 128), jnp.float32)

    row = lax.broadcasted_iota(jnp.int32, (8, 128), 0)
    lane = lax.broadcasted_iota(jnp.int32, (128, 128), 1)

    def neighbours(ref, p):
        v = ref[p + 1]
        total = ref[p] + ref[p + 2]
        above = pltpu.roll(v, 1, 0)
        below = pltpu.roll(v, 127, 0)
        above = jnp.concatenate([jnp.where(row == 0, 0.0, above[:8]), above[8:]], axis=0)
        below = jnp.concatenate([below[:120], jnp.where(row == 7, 0.0, below[120:])], axis=0)
        total = (total + above) + below
        total = total + jnp.where(lane == 0, 0.0, pltpu.roll(v, 1, 1))
        total = total + jnp.where(lane == 127, 0.0, pltpu.roll(v, 127, 1))
        return total, v

    def send(stage, k):
        return pltpu.make_async_remote_copy(
            src_ref=cs.at[stage, k], dst_ref=cr.at[stage, k], send_sem=ss.at[stage, k], recv_sem=rs.at[stage, k],
            device_id={"tm": t + 1}, device_id_type=MESH,
        )

    def halo(ref, stage, side):
        return pltpu.make_async_remote_copy(
            src_ref=ref.at[1 if side == 0 else 16], dst_ref=ref.at[17 if side == 0 else 0],
            send_sem=hs.at[stage, side], recv_sem=hr.at[stage, side],
            device_id={"gx": g - 1 if side == 0 else g + 1}, device_id_type=MESH,
        )

    def start_halos(ref, stage):
        @pl.when(has_left)
        def _():
            halo(ref, stage, 0).start()

        @pl.when(has_right)
        def _():
            halo(ref, stage, 1).start()

    def take_halos(ref, stage):
        @pl.when(has_right)
        def _():
            halo(ref, stage, 0).wait_recv()

        @pl.when(has_left)
        def _():
            halo(ref, stage, 1).wait_recv()

    def start_send(stage, k):
        @pl.when(has_next)
        def _():
            send(stage, k).start()

    def arrive(stage, k):
        @pl.when(has_prev)
        def _():
            send(stage, k).wait_recv()

    def first_rates(k, slot):
        for i, p in enumerate((k, 15 - k)):
            total, v = neighbours(a_v, p)
            rate = mob_v[p] * (total - v * (5.0 + v * v))
            f_v[p] = rate
            e1_v[slot, i] = v + reach * rate

    def first_coefficients(k, slot):
        cs[0, k] = analyse(e1_v[slot, 0], e1_v[slot, 1], tab)

    def start_coefficients(k):
        ca[k] = receives * analyse(a_v[k + 1], a_v[16 - k], tab)

    a_loads[1].wait()
    a_loads[2].wait()
    mob_loads[1].wait()
    mob_loads[2].wait()
    first_rates(FIRST[0], 0)
    a_loads[0].wait()
    a_loads[3].wait()
    pl.semaphore_wait(
        barrier,
        has_left.astype(jnp.int32) + has_right.astype(jnp.int32) + has_prev.astype(jnp.int32) + has_next.astype(jnp.int32),
    )
    start_halos(a_v, 0)
    tab_load.wait()
    for i in range(1, 9):
        if i == 4:
            mob_loads[0].wait()
            mob_loads[3].wait()
            take_halos(a_v, 0)
        if i < 8:
            first_rates(FIRST[i], i % 2)
        first_coefficients(FIRST[i - 1], (i - 1) % 2)
        if i > 1:
            start_coefficients(FIRST[i - 2])
        start_send(0, FIRST[i - 1])
    start_coefficients(FIRST[7])

    def corrected(k):
        for p, plane in zip((k, 15 - k), synthesise(cr[0, k] - ca[k], tab)):
            start = a_v[p + 1] + plane
            ap_v[p] = start
            w_v[p + 1] = q0 * start + s0 * a_v[p + 1] + s1 * f_v[p]

    def second_values(k):
        for p in (k, 15 - k):
            total, w = neighbours(w_v, p)
            a, f, start = a_v[p + 1], f_v[p], ap_v[p]
            square = a * a
            cubes = (s3 * f + (3.0 * s2) * a) * f + (3.0 * s1) * square
            cubes = cubes * f + s0 * (square * a) + q0 * (start * start * start)
            e_v[0, p] = start + (time_step * mob_v[p]) * ((total - 5.0 * w) - cubes)

    def second_coefficients(k):
        cs[1, k] = analyse(e_v[0, k], e_v[0, 15 - k], tab)

    for first, second, third in (
        (7, None, None), (6, None, None), (5, 7, None), (4, 6, 7), (0, 5, 6), (3, None, 5), (2, 4, None), (1, 3, 4),
        (None, 2, 3), (None, 1, 2), (None, 0, 1), (None, None, 0),
    ):
        if first is not None:
            arrive(0, first)
        if second == 0:
            take_halos(w_v, 1)
        if first is not None:
            corrected(first)
        if second is not None:
            second_values(second)
        if third is not None:
            second_coefficients(third)
        if first == 0:
            start_halos(w_v, 1)
        if third is not None:
            start_send(1, third)

    for k in SECOND:
        arrive(1, k)
        for p, plane in zip((k, 15 - k), synthesise(cr[1, k] - cr[0, k], tab)):
            n_v[0, p] = ap_v[p] + plane

    for stage in range(2):
        @pl.when(has_next)
        def _():
            for k in range(8):
                send(stage, k).wait_send()

        ref = (a_v, w_v)[stage]

        @pl.when(has_left)
        def _():
            halo(ref, stage, 0).wait_send()

        @pl.when(has_right)
        def _():
            halo(ref, stage, 1).wait_send()


def store(e_v, n_v, end_hbm, next_hbm, sem):
    copies = [pltpu.make_async_copy(e_v, end_hbm, sem.at[0]), pltpu.make_async_copy(n_v, next_hbm, sem.at[1])]
    for copy in copies:
        copy.start()
    for copy in copies:
        copy.wait()


def body(start_states, mobility):
    plane = (128, 128)
    f32 = jnp.float32
    shape = start_states.shape
    operands = [
        pltpu.with_memory_space_constraint(x, pltpu.HBM) for x in (start_states, mobility, jnp.asarray(tables()))
    ]
    ends = pl.pallas_call(
        kernel,
        out_shape=[pltpu.VMEM(shape, f32)] * 2,
        in_specs=[pl.BlockSpec(memory_space=pltpu.HBM)] * 3,
        out_specs=[pl.BlockSpec(memory_space=pltpu.VMEM)] * 2,
        scratch_shapes=[
            pltpu.VMEM((18,) + plane, f32),
            pltpu.VMEM((16,) + plane, f32),
            pltpu.VMEM((ROWS, 256), jnp.bfloat16),
            pltpu.VMEM((16,) + plane, f32),
            pltpu.VMEM((18,) + plane, f32),
            pltpu.VMEM((16,) + plane, f32),
            pltpu.VMEM((2, 2) + plane, f32),
            pltpu.VMEM((8, 64, 128), f32),
            pltpu.VMEM((2, 8, 64, 128), f32),
            pltpu.VMEM((2, 8, 64, 128), f32),
            pltpu.SemaphoreType.DMA((9,)),
            pltpu.SemaphoreType.DMA((2, 8)),
            pltpu.SemaphoreType.DMA((2, 8)),
            pltpu.SemaphoreType.DMA((2, 2)),
            pltpu.SemaphoreType.DMA((2, 2)),
        ],
        compiler_params=pltpu.CompilerParams(
            collective_id=0, has_side_effects=True, vmem_limit_bytes=32 * 1024 * 1024
        ),
    )(*operands)
    return tuple(pl.pallas_call(
        store,
        out_shape=[jax.ShapeDtypeStruct(shape, f32)] * 2,
        in_specs=[pl.BlockSpec(memory_space=pltpu.VMEM)] * 2,
        out_specs=[pl.BlockSpec(memory_space=pl.ANY)] * 2,
        scratch_shapes=[pltpu.SemaphoreType.DMA((2,))],
    )(*[pltpu.with_memory_space_constraint(x, pltpu.VMEM) for x in ends]))


def solution(mesh):
    placed = (P("tm", "gx", None, None), P("gx", None, None))
    return jax.shard_map(
        body,
        mesh=mesh,
        in_specs=placed,
        out_specs=(P("tm", "gx", None, None), P("tm", "gx", None, None)),
        check_vma=False,
    )
```
